32 devices in a mesh: row: 4 (over x, core), col: 8 (over z, y).
Axes of the slice: x: 2, y: 2, z: 4, core: 2. Of those that a mesh axis runs over, the one named last changes fastest.
Arguments:
- obj: float32 [2, 2, 1024, 2048], P(None, None, 'row', 'col'), may hold values from -1.5 to 1.5
- probe: float32 [2, 256, 256], replicated, may hold values from -5 to 5
- amplitude: float32 [4, 8, 2, 1, 256, 256], P('row', 'col'), may hold values from 0 to 2
- positions: int32 [4, 8, 2, 1, 2], P('row', 'col'), may hold values from 0 to 256
Outputs:
- updated: float32 [2, 2, 1024, 2048], P(None, None, 'row', 'col')
The draws below stay inside these ranges and needn't reach their ends.
Inputs may be any that keep to these rules, and one draw needn't show every extreme that they name: `positions`: every probe window lies inside its tile's region widened by 128 pixels on each side.
All inputs are finite; a program needn't handle non-finite values.
Results may differ from the reference program's by a relative error of at most 0.0003.
Values sent between devices are 32-bit elements; how exact they have to be, the bound alone decides.
No kernel may reach another device: no remote copies, remote signals or barrier semaphores. Data moves between devices by JAX's collectives and lax.ppermute only.
A program may use at most 64 MiB of HBM per device.

```python
import math
import jax
import jax.numpy as jnp
from jax import lax

TILE = 256
MARGIN = 128
PROBES = 1
HEIGHT = 1024
WIDTH = 2048
N_ROW = 4
N_COL = 8


def plant(values, own_key, least, high):
    place = [jax.random.randint(jax.random.fold_in(own_key, axis), (), 0, length) for axis, length in enumerate(values.shape)]
    longest = values.shape.index(max(values.shape))
    next_to = place[:longest] + [(place[longest] + 1) % values.shape[longest]] + place[longest + 1:]
    return values.at[tuple(place)].set(least).at[tuple(next_to)].set(high)


def level_of(key, extent, cuts, low, high):
    gain = 1.0
    for dim, shards_of in cuts:
        heights = jax.random.uniform(jax.random.fold_in(jax.random.fold_in(key, 6), dim), (shards_of,), jnp.float32, low / len(cuts), high / len(cuts))
        gain = gain * jnp.repeat(jnp.exp(heights), extent[dim] // shards_of).reshape((-1,) + (1,) * (len(extent) - 1 - dim))
    return gain


def bell_draw(rng, dims, scale, reach, pieces=(), kind=jnp.bfloat16):
    values = jax.random.normal(rng, dims, jnp.float32) * scale
    if len(pieces) > 0:
        values = level_of(rng, dims, pieces, -0.22, 0.18) * values
    return jnp.clip(values, min=-reach, max=reach).astype(kind)


def setup_inputs(seed: int = 0) -> dict:
    arg_keys = jax.random.split(jax.random.key(seed), 5)
    return {
        "obj": bell_draw(arg_keys[0], (2, 2, HEIGHT, WIDTH), 0.3, 1.5, ((2, 4), (3, 8)), jnp.float32),
        "probe": bell_draw(arg_keys[1], (2, TILE, TILE), 1.0, 5.0, (), jnp.float32),
        "amplitude": jnp.clip(2.0 * jax.random.uniform(arg_keys[2], (N_ROW, N_COL, 2, PROBES, TILE, TILE), jnp.float32) ** level_of(arg_keys[2], (N_ROW, N_COL, 2, PROBES, TILE, TILE), ((0, 4), (1, 8)), -0.2, 0.2), 0.0, 2.0),
        "positions": plant(jax.random.randint(arg_keys[3], (N_ROW, N_COL, 2, PROBES, 2), 0, 2 * MARGIN + 1), jax.random.fold_in(arg_keys[3], 1), 0, 2 * MARGIN).astype(jnp.int32),
    }


step_size = 0.5

def fresnel(size):
    index = jnp.arange(size, dtype=jnp.int32)
    freq = jnp.where(index < size // 2, index, index - size)
    square = (freq[:, None] * freq[:, None] + freq[None, :] * freq[None, :]) % (4 * size)
    phase = math.pi / (2 * size) * square.astype(jnp.float32)
    return jnp.cos(phase) - 1j * jnp.sin(phase)

def probe_gradient(padded_object, exit_wave, propagation_kernel, top_row, left_column, measured):
    zero = jnp.zeros((), jnp.int32)
    patch = lax.dynamic_slice(padded_object, (zero, zero, top_row.astype(jnp.int32), left_column.astype(jnp.int32)), (2, 2, TILE, TILE))
    first = 1.0 + patch[0, 0] + 1j * patch[0, 1]
    second = 1.0 + patch[1, 0] + 1j * patch[1, 1]
    entry = exit_wave * first
    inner = jnp.fft.ifft2(propagation_kernel * jnp.fft.fft2(entry, norm='ortho'), norm='ortho')
    leaving = inner * second
    far = jnp.fft.fft2(leaving, norm='ortho')
    power = far.real * far.real + far.imag * far.imag
    resid = far - measured * far / jnp.sqrt(power + 1.0)
    chi = jnp.fft.ifft2(resid, norm='ortho')
    grad_two = jnp.conj(inner) * chi
    back = jnp.conj(second) * chi
    back = jnp.fft.ifft2(jnp.conj(propagation_kernel) * jnp.fft.fft2(back, norm='ortho'), norm='ortho')
    grad_one = jnp.conj(exit_wave) * back
    return jnp.stack([jnp.stack([grad_one.real, grad_one.imag]), jnp.stack([grad_two.real, grad_two.imag])])

def reference(obj, probe, amplitude, positions):
    padded_object = jnp.pad(obj, ((0, 0), (0, 0), (MARGIN, MARGIN), (MARGIN, MARGIN)))
    propagation_kernel = fresnel(TILE)
    exit_wave = probe[0] + 1j * probe[1]
    result = obj
    for batch in range(2):
        tops = (jnp.arange(N_ROW, dtype=jnp.int32) * TILE)[:, None, None] + positions[:, :, batch, :, 0]
        lefts = (jnp.arange(N_COL, dtype=jnp.int32) * TILE)[None, :, None] + positions[:, :, batch, :, 1]
        tops = tops.reshape(-1).astype(jnp.int32)
        lefts = lefts.reshape(-1).astype(jnp.int32)
        measured = amplitude[:, :, batch].reshape(-1, TILE, TILE)

        def add_one(total, scan_entry):
            top_row, left_column, measured_intensity = scan_entry
            object_gradient = probe_gradient(padded_object, exit_wave, propagation_kernel, top_row, left_column, measured_intensity)
            zero = jnp.zeros((), jnp.int32)
            start = (zero, zero, top_row, left_column)
            current = lax.dynamic_slice(total, start, (2, 2, TILE, TILE))
            return (lax.dynamic_update_slice(total, current + object_gradient.astype(total.dtype), start), None)
        total, unused = lax.scan(add_one, jnp.zeros_like(padded_object), (tops, lefts, measured))
        result = result - step_size * total[:, :, MARGIN:MARGIN + HEIGHT, MARGIN:MARGIN + WIDTH]
    return result
```

```python
import functools

import jax
import jax.numpy as jnp
import numpy as np
from jax import lax
from jax.experimental import pallas as pl
from jax.experimental.pallas import tpu as pltpu
from jax.sharding import PartitionSpec as P

STEP = 0.5
VMEM = pl.BlockSpec(memory_space=pltpu.VMEM)
SMEM = pl.BlockSpec(memory_space=pltpu.SMEM)


def shifted(value, axis, steps):
    count = lax.axis_size(axis)
    first, last = max(0, -steps), min(count, count - steps)
    return lax.ppermute(value, axis, [(i, i + steps) for i in range(first, last)])


def blocks_of(matrix):
    return np.block([[matrix.real, -matrix.imag], [matrix.imag, matrix.real]])


def high_low(values):
    values = values.astype(np.float32)
    high = values.astype(jnp.bfloat16)
    low = (values - high.astype(np.float32)).astype(jnp.bfloat16)
    return np.stack([high, low], 1)


@functools.lru_cache(maxsize=None)
def tables(size):
    half = size // 2
    n = np.arange(half)
    norm = 1.0 / np.sqrt(size)
    even = np.exp(-2j * np.pi * (2 * n[:, None] * n[None, :] % size) / size) * norm
    odd = np.exp(-2j * np.pi * ((2 * n[:, None] + 1) * n[None, :] % size) / size) * norm
    freq = np.where(np.arange(size) < half, np.arange(size), np.arange(size) - size)
    kernel = np.fft.ifft(np.exp(-1j * np.pi * (freq * freq % (4 * size)) / (2 * size)))
    near = kernel[(n[:, None] - n[None, :]) % size]
    far = kernel[(n[:, None] - n[None, :] + half) % size]
    plus, minus = (near + far) / 2, (near - far) / 2
    dft = [even, odd, even.conj().T, odd.conj().T]
    prop = [plus, minus, plus.conj().T, minus.conj().T]
    pair = [high_low(np.stack([blocks_of(m) for m in group])) for group in (dft, prop)]
    return tuple(pair)


def split(x):
    high = x.astype(jnp.bfloat16)
    return high, (x - high.astype(jnp.float32)).astype(jnp.bfloat16)


def dot(a, b):
    return jnp.dot(a, b, preferred_element_type=jnp.float32)


def left(table, k, x):
    high, low = split(x)
    return dot(table[k, 0], high) + dot(table[k, 1], high) + dot(table[k, 0], low)


def right(x, table, k):
    high, low = split(x)
    return dot(high, table[k, 0]) + dot(high, table[k, 1]) + dot(low, table[k, 0])


def cols_in(top, bottom):
    half = top.shape[0] // 2
    sums, diffs = [], []
    for branch in (top, bottom):
        re, im = branch[:half], branch[half:]
        sums.append(jnp.concatenate([re[:, :half] + re[:, half:], im[:, :half] + im[:, half:]], 1))
        diffs.append(jnp.concatenate([re[:, :half] - re[:, half:], im[:, :half] - im[:, half:]], 1))
    return jnp.concatenate(sums, 0), jnp.concatenate(diffs, 0)


def cols_out(first, second):
    half = first.shape[0] // 2
    added, taken = first + second, first - second
    out = []
    for p in (0, 1):
        a, t = added[p * half : (p + 1) * half], taken[p * half : (p + 1) * half]
        re = jnp.concatenate([a[:, :half], t[:, :half]], 1)
        im = jnp.concatenate([a[:, half:], t[:, half:]], 1)
        out.append(jnp.concatenate([re, im], 0))
    return out


def rows_out(top, bottom):
    half = top.shape[0] // 2
    re = jnp.concatenate([top[:half] + bottom[:half], top[:half] - bottom[:half]], 0)
    im = jnp.concatenate([top[half:] + bottom[half:], top[half:] - bottom[half:]], 0)
    return re, im


def rows_in(re, im):
    half = re.shape[0] // 2
    total = jnp.concatenate([re[:half] + re[half:], im[:half] + im[half:]], 0)
    diff = jnp.concatenate([re[:half] - re[half:], im[:half] - im[half:]], 0)
    return total, diff


def propagate(re, im, table, conj):
    a, b = (2, 0) if conj else (0, 2)
    total, diff = rows_in(re, im)
    top, bottom = left(table, a, total), left(table, a + 1, diff)
    sums, diffs = cols_in(top, bottom)
    first, second = right(sums, table, b), right(diffs, table, b + 1)
    return rows_out(*cols_out(first, second))


def masks(spots, index, half):
    rows = lax.broadcasted_iota(jnp.int32, (half, half), 0)
    cols = lax.broadcasted_iota(jnp.int32, (half, half), 1)
    y, x = spots[2 * index], spots[2 * index + 1]
    return [rows + r * half >= y for r in (0, 1)], [cols + c * half >= x for c in (0, 1)]


def picked(parts, plane, row_mask, col_mask):
    own, west, east, north, south, north_ends, south_ends = parts
    half = own.shape[1] // 2

    def block(r, c):
        rows, cols = pl.ds((r - 1) * half, half), pl.ds((c - 1) * half, half)
        if r in (1, 2):
            if c == 0:
                return west[plane, rows, :]
            if c == 3:
                return east[plane, rows, :]
            return own[plane, rows, cols]
        centre, ends = (north, north_ends) if r == 0 else (south, south_ends)
        if c in (1, 2):
            return centre[plane, :, cols]
        return ends[plane, :, pl.ds(0 if c == 0 else half, half)]

    out = []
    for r in (0, 1):
        line = []
        for c in (0, 1):
            upper = jnp.where(col_mask[c], block(r, c), block(r, c + 2))
            lower = jnp.where(col_mask[c], block(r + 2, c), block(r + 2, c + 2))
            line.append(jnp.where(row_mask[r], upper, lower))
        out.append(jnp.concatenate(line, 1))
    return jnp.concatenate(out, 0)


def spread(outs, index, plane, grad, row_mask, col_mask):
    north, middle, south = outs
    half = grad.shape[0] // 2
    for r in (0, 1):
        for c in (0, 1):
            g = grad[r * half : (r + 1) * half, c * half : (c + 1) * half]
            upper, lower = jnp.where(row_mask[r], g, 0.0), jnp.where(row_mask[r], 0.0, g)
            for row, part in ((r, upper), (r + 2, lower)):
                for col in (c, c + 2):
                    value = (
                        jnp.where(col_mask[c], part, 0.0)
                        if col == c
                        else jnp.where(col_mask[c], 0.0, part)
                    )
                    cols = pl.ds(col * half, half)
                    ref, rows = {
                        0: (north, pl.ds(0, half)),
                        1: (middle, pl.ds(0, half)),
                        2: (middle, pl.ds(half, half)),
                        3: (south, pl.ds(0, half)),
                    }[row]
                    if index == 0:
                        ref[plane, rows, cols] = value
                    else:
                        ref[plane, rows, cols] = ref[plane, rows, cols] + value


def three(x):
    high = x.astype(jnp.bfloat16)
    rest = x - high.astype(jnp.float32)
    low = rest.astype(jnp.bfloat16)
    return high, low, (rest - low.astype(jnp.float32)).astype(jnp.bfloat16)


def prepare_kernel(spots, probe, amplitude, probe_out, amp_out):
    count, size = amplitude.shape[0], amplitude.shape[1]
    half = size // 2
    rows = lax.broadcasted_iota(jnp.int32, (size, size), 0)
    cols = lax.broadcasted_iota(jnp.int32, (size, size), 1)

    def ordered(index):
        return jnp.where(index < half, 2 * index, 2 * (index - half) + 1)

    pick_rows = (ordered(rows) == cols).astype(jnp.float32).astype(jnp.bfloat16)
    pick_cols = (ordered(cols) == rows).astype(jnp.float32).astype(jnp.bfloat16)
    for w in range(count):
        for plane in (0, 1):
            rolled = pltpu.roll(probe[plane], spots[2 * w], 0)
            probe_out[w, plane] = pltpu.roll(rolled, spots[2 * w + 1], 1)
        lines = sum(dot(pick_rows, part) for part in three(amplitude[w]))
        amp_out[w] = sum(dot(part, pick_cols) for part in three(lines))


def entry_kernel(spots, own, west, east, north, south, n_ends, s_ends, probe, table, inner):
    parts = (own, west, east, north, south, n_ends, s_ends)
    half = own.shape[1] // 2
    for w in range(probe.shape[0]):
        row_mask, col_mask = masks(spots, w, half)
        re = 1.0 + picked(parts, 0, row_mask, col_mask)
        im = picked(parts, 1, row_mask, col_mask)
        p_re, p_im = probe[w, 0], probe[w, 1]
        out = propagate(p_re * re - p_im * im, p_re * im + p_im * re, table, False)
        inner[w, 0], inner[w, 1] = out


def middle_kernel(
    spots, own, west, east, north, south, n_ends, s_ends, inner, amp, table, back, gn, gm, gs
):
    parts = (own, west, east, north, south, n_ends, s_ends)
    size = own.shape[1]
    half = size // 2
    for w in range(inner.shape[0]):
        row_mask, col_mask = masks(spots, w, half)
        t_re = 1.0 + picked(parts, 0, row_mask, col_mask)
        t_im = picked(parts, 1, row_mask, col_mask)
        b_re, b_im = inner[w, 0], inner[w, 1]
        total, diff = rows_in(b_re * t_re - b_im * t_im, b_re * t_im + b_im * t_re)
        top, bottom = left(table, 0, total), left(table, 1, diff)
        sums, diffs = cols_in(top, bottom)
        resid = []
        for q, (data, k) in enumerate(((sums, 2), (diffs, 3))):
            far = right(data, table, k)
            f_re, f_im = far[:, :half], far[:, half:]
            measured = amp[w, :, pl.ds(q * half, half)]
            factor = 1.0 - measured * lax.rsqrt(f_re * f_re + f_im * f_im + 1.0)
            resid.append(jnp.concatenate([f_re * factor, f_im * factor], 1))
        first, second = right(resid[0], table, 0), right(resid[1], table, 1)
        top, bottom = cols_out(first, second)
        c_re, c_im = rows_out(left(table, 2, top), left(table, 3, bottom))
        spread((gn, gm, gs), w, 0, b_re * c_re + b_im * c_im, row_mask, col_mask)
        spread((gn, gm, gs), w, 1, b_re * c_im - b_im * c_re, row_mask, col_mask)
        back[w, 0] = t_re * c_re + t_im * c_im
        back[w, 1] = t_re * c_im - t_im * c_re


def exit_kernel(spots, back, probe, table, gn, gm, gs):
    half = back.shape[2] // 2
    for w in range(back.shape[0]):
        row_mask, col_mask = masks(spots, w, half)
        b_re, b_im = propagate(back[w, 0], back[w, 1], table, True)
        p_re, p_im = probe[w, 0], probe[w, 1]
        spread((gn, gm, gs), w, 0, p_re * b_re + p_im * b_im, row_mask, col_mask)
        spread((gn, gm, gs), w, 1, p_re * b_im - p_im * b_re, row_mask, col_mask)


def kernel_call(kernel, shapes, specs, flops):
    return pl.pallas_call(
        kernel,
        out_shape=[jax.ShapeDtypeStruct(s, jnp.float32) for s in shapes],
        in_specs=[SMEM] + [VMEM] * specs,
        out_specs=[VMEM] * len(shapes),
        cost_estimate=pl.CostEstimate(flops=flops, bytes_accessed=1 << 21, transcendentals=0),
    )


def body(obj, probe, amplitude, positions):
    size = probe.shape[1]
    half = size // 2
    spots = positions.reshape(-1)
    measured = amplitude.reshape(-1, size, size)
    count = measured.shape[0]
    dft, prop = (jnp.asarray(t) for t in tables(size))

    sides = []
    for s in (0, 1):
        east = shifted(obj[s, :, :, :half], "col", -1)
        west = shifted(obj[s, :, :, half:], "col", 1)
        sides.append((west, east))
    north = shifted(obj[:, :, half:, :], "row", 1)
    south = shifted(obj[:, :, :half, :], "row", -1)
    parts = []
    for s in (0, 1):
        west, east = sides[s]
        lower = jnp.concatenate([west[:, half:, :], east[:, half:, :]], 2)
        upper = jnp.concatenate([west[:, :half, :], east[:, :half, :]], 2)
        ends = shifted(lower, "row", 1), shifted(upper, "row", -1)
        parts.append((obj[s], west, east, north[s], south[s], *ends))

    field = (count, 2, size, size)
    flop = 6 * 2 * size**3 * 2 * count
    rolled, amp = kernel_call(prepare_kernel, [field, (count, size, size)], 2, flop)(
        spots, probe, measured
    )
    (inner,) = kernel_call(entry_kernel, [field], 9, 2 * flop)(spots, *parts[0], rolled, prop)
    grads = [(2, half, 2 * size), (2, size, 2 * size), (2, half, 2 * size)]
    back, *second = kernel_call(middle_kernel, [field] + grads, 10, 4 * flop)(
        spots, *parts[1], inner, amp, dft
    )
    first = kernel_call(exit_kernel, grads, 3, 2 * flop)(spots, back, rolled, prop)

    outs = []
    for s, (gn, gm, gs) in ((1, second), (0, first)):
        from_south = shifted(gn, "row", -1)
        from_north = shifted(gs, "row", 1)
        total = gm + jnp.concatenate([from_north, from_south], 1)
        from_east = shifted(total[:, :, :half], "col", -1)
        from_west = shifted(total[:, :, size + half :], "col", 1)
        both = total[:, :, half : half + size] + jnp.concatenate([from_west, from_east], 2)
        outs.append(obj[s] - STEP * both)
    return jnp.stack([outs[1], outs[0]])


def solution(mesh):
    placed = (
        P(None, None, "row", "col"),
        P(),
        P("row", "col", None, None, None, None),
        P("row", "col", None, None, None),
    )
    return jax.shard_map(
        body, mesh=mesh, in_specs=placed, out_specs=P(None, None, "row", "col"), check_vma=False
    )
```
